32 devices in a mesh: doc: 8 (over z, x), bkt: 4 (over y, core).
Axes of the slice: x: 2, y: 2, z: 4, core: 2. Of those that a mesh axis runs over, the one named last changes fastest.
Arguments:
- start_vectors: float32 [64, 32768], P(None, ('doc', 'bkt')), may hold values from -6 to 6
- bucket_weight: float32 [8192], P('bkt'), may hold values from 0.1 to 1
- tile_count: int32 [8, 4], P('doc', 'bkt'), may hold values from 128 to 256, as said below
- tile_coords: int32 [8, 4, 256, 2], P('doc', 'bkt'), may hold values from 0 to 31, as said below
- patterns: int32 [8, 4, 256, 128, 128], P('doc', 'bkt'), may hold values from 0 to 1
Outputs:
- eigen_block: float32 [64, 32768], P(None, ('doc', 'bkt'))
The draws below stay inside these ranges and needn't reach their ends.
Inputs may be any that keep to these rules, and one draw needn't show every extreme that they name: `tile_count`: the largest count is exactly 256 in every draw. `tile_coords`: row tiles lie below 32, column tiles below 16; the pairs of one document band and bucket band are distinct.
All inputs are finite; a program needn't handle non-finite values.
Results may differ from the reference program's by a relative error of at most 0.018.
Values may be sent and summed in bfloat16 or wider, within the bound.
A program may use at most 128 MiB of HBM per device.

```python
import math
import jax
import jax.numpy as jnp
from jax import lax

K = 64
TILE = 128
ITERS = 2
DOC_BAND = 4096
TMAX = 256
DOC_BANDS = 8
BKT_BANDS = 4
BKT_BAND = 2048
NDOC = 32768
NBKT = 8192


def draw_tile_count(key, part):
    device_total = DOC_BANDS * BKT_BANDS
    base = jax.random.randint(jax.random.fold_in(key, 21), (device_total,), TMAX // 2, TMAX + 1)
    fullest = jax.random.randint(jax.random.fold_in(key, 22), (), 0, device_total)
    counts = jnp.where(jnp.arange(device_total) == fullest, TMAX, base)
    return counts.reshape(DOC_BANDS, BKT_BANDS).astype(jnp.int32)


def draw_tile_coords(key, part):
    row_tiles = DOC_BAND // TILE
    col_tiles = BKT_BAND // TILE
    keys = jax.random.split(jax.random.fold_in(key, 11), DOC_BANDS * BKT_BANDS)
    picks = jax.vmap(lambda single: jax.random.permutation(single, row_tiles * col_tiles)[:TMAX])(keys)
    coords = jnp.stack([picks // col_tiles, picks % col_tiles], axis=-1)
    return coords.reshape(DOC_BANDS, BKT_BANDS, TMAX, 2).astype(jnp.int32)


def draw_patterns(key, part):
    shape_rows = (DOC_BANDS, BKT_BANDS, TMAX, TILE, 1)
    shape_full = (DOC_BANDS, BKT_BANDS, TMAX, TILE, TILE)
    levels = jax.random.randint(jax.random.fold_in(key, 31), shape_rows, 1, 17)
    values = jax.random.randint(jax.random.fold_in(key, 32), shape_full, 0, 256)
    return (values < levels).astype(jnp.int32)


def shard_levels(key, dims, shards, low, largest):
    level = 1.0
    for axis_at, blocks in shards:
        draws = jax.random.uniform(jax.random.fold_in(jax.random.fold_in(key, 6), axis_at), (blocks,), jnp.float32, low / len(shards), largest / len(shards))
        level = level * jnp.repeat(jnp.exp(draws), dims[axis_at] // blocks).reshape((-1,) + (1,) * (len(dims) - 1 - axis_at))
    return level


def gaussian(key, extent, width, reach, cuts=(), kind=jnp.bfloat16):
    drawn = width * jax.random.normal(key, extent, jnp.float32)
    if cuts:
        drawn = drawn * shard_levels(key, extent, cuts, -0.22, 0.18)
    return jnp.clip(drawn, -reach, reach).astype(kind)


def setup_inputs(seed: int = 0) -> dict:
    key_list = jax.random.split(jax.random.key(seed), 6)
    start_vectors = gaussian(key_list[0], (K, NDOC), 1.0, 6.0, ((1, 32),), jnp.float32)
    bucket_weight = jnp.clip(jnp.exp(math.log(1.0) - 2.3025851 * jax.random.uniform(key_list[1], (NBKT,), jnp.float32) ** shard_levels(key_list[1], (NBKT,), ((0, 4),), -0.2, 0.2)), 0.1, 1.0)
    tile_count = draw_tile_count(jax.random.fold_in(key_list[5], 71), 0)
    tile_coords = draw_tile_coords(jax.random.fold_in(key_list[5], 71), 0)
    patterns = draw_patterns(jax.random.fold_in(key_list[5], 71), 0)
    return dict(start_vectors=start_vectors, bucket_weight=bucket_weight, tile_count=tile_count, tile_coords=tile_coords, patterns=patterns)


def reference(start_vectors, bucket_weight, tile_count, tile_coords, patterns):
    row_tiles = DOC_BAND // TILE
    col_tiles = BKT_BAND // TILE
    device_total = DOC_BANDS * BKT_BANDS
    band_doc = jnp.repeat(jnp.arange(DOC_BANDS, dtype=jnp.int32), BKT_BANDS)
    band_bkt = jnp.tile(jnp.arange(BKT_BANDS, dtype=jnp.int32), DOC_BANDS)
    coords = tile_coords.reshape(device_total, TMAX, 2)
    global_rows = (band_doc[:, None] * row_tiles + coords[:, :, 0]).astype(jnp.int32)
    global_cols = (band_bkt[:, None] * col_tiles + coords[:, :, 1]).astype(jnp.int32)
    live_slot = jnp.arange(TMAX, dtype=jnp.int32)[None, :] < tile_count.reshape(device_total)[:, None]
    tiles_all = patterns.reshape(device_total, TMAX, TILE, TILE)
    items = (tiles_all, global_rows, global_cols, live_slot)
    weight_tiles = bucket_weight.reshape(NBKT // TILE, TILE)

    def masked_tiles(tiles, live):
        return jnp.where(live[:, None, None], tiles, 0).astype(jnp.float32)

    def degree_step(carry, item):
        doc_sum, bucket_sum = carry
        tiles, rows, cols, live = item
        masked = masked_tiles(tiles, live)
        row_part = jnp.einsum('tij,tj->ti', masked, weight_tiles[cols], precision=lax.Precision.HIGHEST)
        doc_sum = doc_sum.at[rows].add(row_part)
        bucket_sum = bucket_sum.at[cols].add(lax.optimization_barrier(jnp.sum(masked, axis=1)))
        return ((doc_sum, bucket_sum), None)
    start = (jnp.zeros((NDOC // TILE, TILE), jnp.float32), jnp.zeros((NBKT // TILE, TILE), jnp.float32))
    (doc_sum, bucket_sum), _ = lax.scan(degree_step, start, items)
    inv_doc = 1.0 / jnp.sqrt(jnp.maximum(doc_sum.reshape(NDOC), 1.0))
    bucket_scale = bucket_weight / jnp.maximum(bucket_sum.reshape(NBKT), 1.0)
    block = start_vectors
    for sweep_index in range(ITERS):
        scaled = (block * inv_doc[None, :]).astype(jnp.bfloat16)
        scaled_tiles = scaled.reshape(K, NDOC // TILE, TILE)

        def forward_step(carry, item):
            tiles, rows, cols, live = item
            masked = masked_tiles(tiles, live)
            picked = scaled_tiles[:, rows, :].astype(jnp.float32)
            terms = jnp.einsum('kti,tij->ktj', picked, masked, precision=lax.Precision.HIGHEST)
            return (carry.at[:, cols, :].add(terms), None)
        panel, _ = lax.scan(forward_step, jnp.zeros((K, NBKT // TILE, TILE), jnp.float32), items)
        weighted = (panel.reshape(K, NBKT) * bucket_scale[None, :]).astype(jnp.bfloat16)
        weighted_tiles = weighted.reshape(K, NBKT // TILE, TILE)

        def backward_step(carry, item):
            tiles, rows, cols, live = item
            masked = masked_tiles(tiles, live)
            picked = weighted_tiles[:, cols, :].astype(jnp.float32)
            terms = jnp.einsum('ktj,tij->kti', picked, masked, precision=lax.Precision.HIGHEST)
            return (carry.at[:, rows, :].add(terms), None)
        image, _ = lax.scan(backward_step, jnp.zeros((K, NDOC // TILE, TILE), jnp.float32), items)
        image = image.reshape(K, NDOC) * inv_doc[None, :]
        gram_matrix = jnp.dot(image, image.T, precision=lax.Precision.HIGHEST) / NDOC
        factor = jnp.linalg.cholesky(gram_matrix)
        block = lax.linalg.triangular_solve(factor, image, left_side=True, lower=True)
    return block
```

```python
import functools

import jax
import jax.numpy as jnp
from jax import lax
from jax.experimental import pallas as pl
from jax.experimental.pallas import tpu as pltpu
from jax.sharding import PartitionSpec as P

ITERS = 2


def plain_body(start_vectors, bucket_weight, tile_count, tile_coords, patterns):
    highest = lax.Precision.HIGHEST
    slot_total = patterns.shape[2]
    tile_size = patterns.shape[3]
    vector_count = start_vectors.shape[0]
    own_rows = start_vectors.shape[1]
    band_rows = own_rows * lax.axis_size("bkt")
    band_cols = bucket_weight.shape[0]
    row_tiles = band_rows // tile_size
    col_tiles = band_cols // tile_size
    total_docs = band_rows * lax.axis_size("doc")
    live_slot = (jnp.arange(slot_total) < tile_count[0, 0]).astype(jnp.int32)
    pattern_int = patterns[0, 0] * live_slot[:, None, None]
    pattern = pattern_int.astype(jnp.bfloat16)
    row_index = tile_coords[0, 0, :, 0]
    col_index = tile_coords[0, 0, :, 1]
    row_pick = jnp.arange(row_tiles)[:, None] == row_index[None, :]
    col_pick = jnp.arange(col_tiles)[:, None] == col_index[None, :]
    row_pick_f = row_pick.astype(jnp.float32)
    row_pick_b = row_pick.astype(jnp.bfloat16)
    col_pick_f = col_pick.astype(jnp.float32)
    col_pick_b = col_pick.astype(jnp.bfloat16)
    pattern_f = pattern_int.astype(jnp.float32)
    weight_tiles = bucket_weight.reshape(col_tiles, tile_size)
    slot_weight = jnp.dot(col_pick_f.T, weight_tiles, precision=highest)
    row_part = jnp.einsum("tij,tj->ti", pattern_f, slot_weight, precision=highest)
    doc_part = jnp.dot(row_pick_f, row_part, precision=highest).reshape(band_rows)
    col_part = jnp.sum(pattern_f, axis=1)
    bucket_part = jnp.dot(col_pick_f, col_part, precision=highest).reshape(band_cols)
    doc_degree = lax.psum(doc_part, "bkt")
    bucket_size = lax.psum(bucket_part.astype(jnp.bfloat16), "doc").astype(jnp.float32)
    inv_band = 1.0 / jnp.sqrt(jnp.maximum(doc_degree, 1.0))
    inv_own = lax.dynamic_slice_in_dim(inv_band, lax.axis_index("bkt") * own_rows, own_rows)
    bucket_scale = bucket_weight / jnp.maximum(bucket_size, 1.0)
    vectors = start_vectors
    for sweep_index in range(ITERS):
        scaled = (vectors * inv_own[None, :]).astype(jnp.bfloat16)
        band_vecs = lax.all_gather(scaled, "bkt", axis=1, tiled=True)
        picked = jnp.einsum(
            "rt,kri->kti",
            row_pick_b,
            band_vecs.reshape(vector_count, row_tiles, tile_size),
            preferred_element_type=jnp.float32,
        ).astype(jnp.bfloat16)
        products = jnp.einsum("kti,tij->ktj", picked, pattern, preferred_element_type=jnp.float32)
        panel_part = (
            jnp.zeros((vector_count, col_tiles, tile_size), jnp.float32)
            .at[:, col_index, :]
            .add(products)
        )
        panel_part = panel_part.reshape(vector_count, band_cols)
        panel_whole = lax.psum(panel_part, "doc")
        weighted = (panel_whole * bucket_scale[None, :]).astype(jnp.bfloat16)
        spread = jnp.einsum(
            "ct,kcj->ktj",
            col_pick_b,
            weighted.reshape(vector_count, col_tiles, tile_size),
            preferred_element_type=jnp.float32,
        ).astype(jnp.bfloat16)
        returned = jnp.einsum("ktj,tij->kti", spread, pattern, preferred_element_type=jnp.float32)
        row_terms = (
            jnp.zeros((vector_count, row_tiles, tile_size), jnp.float32)
            .at[:, row_index, :]
            .add(returned)
        )
        row_terms = row_terms.reshape(vector_count, band_rows)
        rows_own = (
            lax.psum_scatter(row_terms, "bkt", scatter_dimension=1, tiled=True) * inv_own[None, :]
        )
        gram_local = jnp.dot(rows_own, rows_own.T, precision=highest)
        gram_matrix = lax.psum(gram_local, ("doc", "bkt")) / total_docs
        factor = jnp.linalg.cholesky(gram_matrix)
        vectors = lax.linalg.triangular_solve(factor, rows_own, left_side=True, lower=True)
    return vectors


MESH = pl.DeviceIdType.MESH
F32 = jnp.float32
BF16 = jnp.bfloat16
NT = (((1,), (1,)), ((), ()))


def kernel(
    nd,
    nb,
    slot_ref,
    live_ref,
    start_ref,
    weight_ref,
    patterns_hbm,
    out_ref,
    tiles,
    dense,
    doc_part,
    doc_recv,
    size_part,
    size_recv,
    band,
    panel_send,
    panel_recv,
    weighted,
    image_acc,
    image_send,
    image_recv,
    gram_one,
    gram_one_recv,
    gram_two,
    gram_two_recv,
    load_sem,
    deg_send_sem,
    deg_recv_sem,
    size_send_sem,
    size_recv_sem,
    band_send_sem,
    band_recv_sem,
    panel_send_sem,
    panel_recv_sem,
    wt_send_sem,
    wt_recv_sem,
    image_send_sem,
    image_recv_sem,
    g1_send_sem,
    g1_recv_sem,
    g2_send_sem,
    g2_recv_sem,
):
    highest = lax.Precision.HIGHEST
    me_d = lax.axis_index("doc")
    me_b = lax.axis_index("bkt")
    tile = tiles.shape[1]
    k_vec, own_rows = start_ref.shape
    own_cols = dense.shape[2]
    row_tiles = dense.shape[1] // tile
    col_per = own_cols // tile
    col_tiles = nd * col_per
    tiles_per_own = own_rows // tile
    total_docs = own_rows * nb * nd

    def d_peer(k):
        return {"doc": lax.rem(me_d + k, nd)}

    def b_peer(k):
        return {"bkt": lax.rem(me_b + k, nb)}

    load = pltpu.make_async_copy(patterns_hbm, tiles, load_sem)
    load.start()
    barrier = pltpu.get_barrier_semaphore()
    for k in range(1, nb):
        pl.semaphore_signal(barrier, inc=1, device_id=b_peer(k), device_id_type=MESH)
    for k in range(1, nd):
        pl.semaphore_signal(barrier, inc=1, device_id=d_peer(k), device_id_type=MESH)
    pl.semaphore_wait(barrier, nb + nd - 2)
    load.wait()

    def remote(src, dst, ssem, rsem, peer):
        copy = pltpu.make_async_remote_copy(
            src_ref=src, dst_ref=dst, send_sem=ssem, recv_sem=rsem,
            device_id=peer, device_id_type=MESH,
        )
        copy.start()
        return copy

    size_part[...] = jnp.zeros_like(size_part)

    @pl.loop(0, row_tiles)
    def _(r):
        total = jnp.zeros((tile, tile), F32)
        for c in range(col_tiles):
            o, h = c // col_per, c % col_per
            lanes = slice(h * tile, (h + 1) * tile)
            at = r * col_tiles + c
            block = tiles[slot_ref[at]].astype(F32) * live_ref[at]
            dense[o, pl.ds(pl.multiple_of(r * tile, tile), tile), lanes] = block.astype(BF16)
            size_part[o, :, lanes] += jnp.sum(block, axis=0, keepdims=True)
            total = total + block * weight_ref[o, :, lanes]
        summed = jnp.sum(total.T, axis=0, keepdims=True)
        doc_part[r // tiles_per_own, :, pl.ds(pl.multiple_of(lax.rem(r, tiles_per_own) * tile, tile), tile)] = summed

    copies = []
    for k in range(1, nb):
        q = lax.rem(me_b + k, nb)
        copies.append(remote(doc_part.at[q], doc_recv.at[k], deg_send_sem.at[k], deg_recv_sem.at[k], b_peer(k)))
    for k in range(1, nd):
        o = lax.rem(me_d + k, nd)
        copies.append(remote(size_part.at[o], size_recv.at[k], size_send_sem.at[k], size_recv_sem.at[k], d_peer(k)))
    for copy in copies:
        copy.wait()
    degree = doc_part[me_b]
    for k in range(1, nb):
        degree = degree + doc_recv[k]
    size = size_part[me_d]
    for k in range(1, nd):
        size = size + size_recv[k]
    inv_own = 1.0 / jnp.sqrt(jnp.maximum(degree, 1.0))
    scale = weight_ref[me_d] / jnp.maximum(size, 1.0)

    vectors = start_ref[...]
    for it in range(ITERS):
        band[it, 0] = (vectors * inv_own).astype(BF16)
        sent = [
            remote(band.at[it, 0], band.at[it, k], band_send_sem.at[it, k], band_recv_sem.at[it, k], b_peer(k))
            for k in range(1, nb)
        ]
        for copy in sent:
            copy.wait()

        def panel_of(o):
            acc = jnp.zeros((k_vec, own_cols), F32)
            for k in range(nb):
                source = lax.rem(me_b - k + nb, nb)
                rows = pl.ds(pl.multiple_of(source * own_rows, own_rows), own_rows)
                acc = acc + jnp.dot(band[it, k], dense[o, rows, :], preferred_element_type=F32)
            return acc

        @pl.loop(1, nd)
        def _(k):
            panel_send[it, k] = panel_of(lax.rem(me_d + k, nd)).astype(BF16)
            remote(panel_send.at[it, k], panel_recv.at[it, k], panel_send_sem.at[it, k], panel_recv_sem.at[it, k], d_peer(k))

        whole = panel_of(me_d)
        for k in range(1, nd):
            pltpu.make_async_remote_copy(
                src_ref=panel_send.at[it, k], dst_ref=panel_recv.at[it, k],
                send_sem=panel_send_sem.at[it, k], recv_sem=panel_recv_sem.at[it, k],
                device_id=d_peer(k), device_id_type=MESH,
            ).wait()
            whole = whole + panel_recv[it, k].astype(F32)
        weighted[it, 0] = (whole * scale).astype(BF16)
        sent = [
            remote(weighted.at[it, 0], weighted.at[it, k], wt_send_sem.at[it, k], wt_recv_sem.at[it, k], d_peer(k))
            for k in range(1, nd)
        ]
        for copy in sent:
            copy.wait()

        def image_of(q):
            rows = pl.ds(pl.multiple_of(q * own_rows, own_rows), own_rows)
            image_acc[...] = lax.dot_general(weighted[it, 0], dense[me_d, rows, :], NT, preferred_element_type=F32)

            @pl.loop(1, nd)
            def _(k):
                source = lax.rem(me_d - k + nd, nd)
                image_acc[...] += lax.dot_general(weighted[it, k], dense[source, rows, :], NT, preferred_element_type=F32)

        sent = []
        for k in range(1, nb):
            image_of(lax.rem(me_b + k, nb))
            image_send[it, k] = image_acc[...].astype(BF16)
            sent.append(
                remote(image_send.at[it, k], image_recv.at[it, k], image_send_sem.at[it, k], image_recv_sem.at[it, k], b_peer(k))
            )
        image_of(me_b)
        for copy in sent:
            copy.wait()
        image = image_acc[...]
        for k in range(1, nb):
            image = image + image_recv[it, k].astype(F32)
        image = image * inv_own

        gram = lax.dot_general(image, image, NT, precision=highest, preferred_element_type=F32)
        half = k_vec // 2
        gram_one[it] = jnp.concatenate([gram[:half], gram[half:]], axis=1)
        sent = [
            remote(gram_one.at[it], gram_one_recv.at[it, k], g1_send_sem.at[it, k], g1_recv_sem.at[it, k], b_peer(k))
            for k in range(1, nb)
        ]
        folded = gram_one[it]
        for k in range(1, nb):
            sent[k - 1].wait()
            folded = folded + gram_one_recv[it, k]
        gram_two[it] = folded
        sent = [
            remote(gram_two.at[it], gram_two_recv.at[it, k], g2_send_sem.at[it, k], g2_recv_sem.at[it, k], d_peer(k))
            for k in range(1, nd)
        ]
        for k in range(1, nd):
            sent[k - 1].wait()
            folded = folded + gram_two_recv[it, k]
        gram = jnp.concatenate([folded[:, :k_vec], folded[:, k_vec:]], axis=0) / total_docs

        row_at = lax.broadcasted_iota(jnp.int32, (k_vec, k_vec), 0)
        col_at = lax.broadcasted_iota(jnp.int32, (k_vec, k_vec), 1)
        eye = (row_at == col_at).astype(F32)
        work = jnp.concatenate([gram, eye], axis=1)
        below = lax.broadcasted_iota(jnp.int32, (k_vec, 1), 0)
        pivots = jnp.zeros((k_vec, 1), F32)
        for j in range(k_vec):
            pivot = work[j : j + 1, j : j + 1]
            pivots = jnp.where(below == j, pivot, pivots)
            if j + 1 < k_vec:
                factor = jnp.where(below > j, work[:, j : j + 1] / pivot, 0.0)
                work = work - factor * work[j : j + 1, :]
        inverse = work[:, k_vec:] / jnp.sqrt(pivots)
        vectors = jnp.dot(inverse, image, precision=highest, preferred_element_type=F32)
    out_ref[...] = vectors


def scratch_of(nd, nb, slots, tile, k_vec, own_rows, own_cols):
    dma = pltpu.SemaphoreType.DMA
    vmem = pltpu.VMEM
    fold = (k_vec // 2, 2 * k_vec)
    buffers = [
        ((slots, tile, tile), jnp.int32),
        ((nd, own_rows * nb, own_cols), BF16),
        ((nb, 1, own_rows), F32),
        ((nb, 1, own_rows), F32),
        ((nd, 1, own_cols), F32),
        ((nd, 1, own_cols), F32),
        ((ITERS, nb, k_vec, own_rows), BF16),
        ((ITERS, nd, k_vec, own_cols), BF16),
        ((ITERS, nd, k_vec, own_cols), BF16),
        ((ITERS, nd, k_vec, own_cols), BF16),
        ((k_vec, own_rows), F32),
        ((ITERS, nb, k_vec, own_rows), BF16),
        ((ITERS, nb, k_vec, own_rows), BF16),
        ((ITERS,) + fold, F32),
        ((ITERS, nb) + fold, F32),
        ((ITERS,) + fold, F32),
        ((ITERS, nd) + fold, F32),
    ]
    total = 0
    for shape, kind in buffers:
        count = jnp.dtype(kind).itemsize
        for extent in shape:
            count *= extent
        total += count
    sems = [dma]
    sems += [dma((nb,))] * 2 + [dma((nd,))] * 2
    sems += [dma((ITERS, nb))] * 2 + [dma((ITERS, nd))] * 4
    sems += [dma((ITERS, nb))] * 4 + [dma((ITERS, nd))] * 2
    return [vmem(shape, kind) for shape, kind in buffers] + sems, total


VMEM_BYTES = 60000 * 1024


def body(start_vectors, bucket_weight, tile_count, tile_coords, patterns):
    nd, nb = lax.axis_size("doc"), lax.axis_size("bkt")
    slots, tile = patterns.shape[2], patterns.shape[3]
    k_vec, own_rows = start_vectors.shape
    band_cols = bucket_weight.shape[0]
    own_cols = band_cols // nd
    scratch, total = scratch_of(nd, nb, slots, tile, k_vec, own_rows, own_cols)
    fits = total + 6 * k_vec * own_rows * 4 < VMEM_BYTES
    even = band_cols % (nd * tile) == 0 and own_rows % tile == 0 and 2 * k_vec == tile
    if not (fits and even):
        return plain_body(start_vectors, bucket_weight, tile_count, tile_coords, patterns)
    row_tiles, col_tiles = own_rows * nb // tile, band_cols // tile
    places = tile_coords[0, 0, :, 0] * col_tiles + tile_coords[0, 0, :, 1]
    slot_ids = jnp.arange(slots)
    places = jnp.where(slot_ids < tile_count[0, 0], places, -1)
    match = jnp.arange(row_tiles * col_tiles)[:, None] == places[None, :]
    found = jnp.max(jnp.where(match, slot_ids[None, :], -1), axis=1)
    live = (found >= 0).astype(F32)
    slot_of = jnp.maximum(found, 0).astype(jnp.int32)
    smem = pl.BlockSpec(memory_space=pltpu.SMEM)
    vmem = pl.BlockSpec(memory_space=pltpu.VMEM)
    return pl.pallas_call(
        functools.partial(kernel, nd, nb),
        out_shape=jax.ShapeDtypeStruct((k_vec, own_rows), F32),
        in_specs=[smem, smem, vmem, vmem, pl.BlockSpec(memory_space=pl.ANY)],
        out_specs=vmem,
        scratch_shapes=scratch,
        compiler_params=pltpu.CompilerParams(
            collective_id=0, has_side_effects=True, vmem_limit_bytes=VMEM_BYTES
        ),
        name="subspace",
    )(slot_of, live, start_vectors, bucket_weight.reshape(nd, 1, own_cols), patterns.reshape(slots, tile, tile))


def solution(mesh):
    in_specs = (
        P(None, ("doc", "bkt")),
        P("bkt"),
        P("doc", "bkt"),
        P("doc", "bkt", None, None),
        P("doc", "bkt", None, None, None),
    )
    out_specs = P(None, ("doc", "bkt"))
    return jax.shard_map(body, mesh=mesh, in_specs=in_specs, out_specs=out_specs, check_vma=False)
```

```python
import functools

import jax
import jax.numpy as jnp
from jax import lax
from jax.experimental import pallas as pl
from jax.experimental.pallas import tpu as pltpu
from jax.sharding import PartitionSpec as P

ITERS = 2


def plain_body(start_vectors, bucket_weight, tile_count, tile_coords, patterns):
    highest = lax.Precision.HIGHEST
    slot_total = patterns.shape[2]
    tile_size = patterns.shape[3]
    vector_count = start_vectors.shape[0]
    own_rows = start_vectors.shape[1]
    band_rows = own_rows * lax.axis_size("bkt")
    band_cols = bucket_weight.shape[0]
    row_tiles = band_rows // tile_size
    col_tiles = band_cols // tile_size
    total_docs = band_rows * lax.axis_size("doc")
    live_slot = (jnp.arange(slot_total) < tile_count[0, 0]).astype(jnp.int32)
    pattern_int = patterns[0, 0] * live_slot[:, None, None]
    pattern = pattern_int.astype(jnp.bfloat16)
    row_index = tile_coords[0, 0, :, 0]
    col_index = tile_coords[0, 0, :, 1]
    row_pick = jnp.arange(row_tiles)[:, None] == row_index[None, :]
    col_pick = jnp.arange(col_tiles)[:, None] == col_index[None, :]
    row_pick_f = row_pick.astype(jnp.float32)
    row_pick_b = row_pick.astype(jnp.bfloat16)
    col_pick_f = col_pick.astype(jnp.float32)
    col_pick_b = col_pick.astype(jnp.bfloat16)
    pattern_f = pattern_int.astype(jnp.float32)
    weight_tiles = bucket_weight.reshape(col_tiles, tile_size)
    slot_weight = jnp.dot(col_pick_f.T, weight_tiles, precision=highest)
    row_part = jnp.einsum("tij,tj->ti", pattern_f, slot_weight, precision=highest)
    doc_part = jnp.dot(row_pick_f, row_part, precision=highest).reshape(band_rows)
    col_part = jnp.sum(pattern_f, axis=1)
    bucket_part = jnp.dot(col_pick_f, col_part, precision=highest).reshape(band_cols)
    doc_degree = lax.psum(doc_part, "bkt")
    bucket_size = lax.psum(bucket_part.astype(jnp.bfloat16), "doc").astype(jnp.float32)
    inv_band = 1.0 / jnp.sqrt(jnp.maximum(doc_degree, 1.0))
    inv_own = lax.dynamic_slice_in_dim(inv_band, lax.axis_index("bkt") * own_rows, own_rows)
    bucket_scale = bucket_weight / jnp.maximum(bucket_size, 1.0)
    vectors = start_vectors
    for sweep_index in range(ITERS):
        scaled = (vectors * inv_own[None, :]).astype(jnp.bfloat16)
        band_vecs = lax.all_gather(scaled, "bkt", axis=1, tiled=True)
        picked = jnp.einsum(
            "rt,kri->kti",
            row_pick_b,
            band_vecs.reshape(vector_count, row_tiles, tile_size),
            preferred_element_type=jnp.float32,
        ).astype(jnp.bfloat16)
        products = jnp.einsum("kti,tij->ktj", picked, pattern, preferred_element_type=jnp.float32)
        panel_part = (
            jnp.zeros((vector_count, col_tiles, tile_size), jnp.float32)
            .at[:, col_index, :]
            .add(products)
        )
        panel_part = panel_part.reshape(vector_count, band_cols)
        panel_whole = lax.psum(panel_part, "doc")
        weighted = (panel_whole * bucket_scale[None, :]).astype(jnp.bfloat16)
        spread = jnp.einsum(
            "ct,kcj->ktj",
            col_pick_b,
            weighted.reshape(vector_count, col_tiles, tile_size),
            preferred_element_type=jnp.float32,
        ).astype(jnp.bfloat16)
        returned = jnp.einsum("ktj,tij->kti", spread, pattern, preferred_element_type=jnp.float32)
        row_terms = (
            jnp.zeros((vector_count, row_tiles, tile_size), jnp.float32)
            .at[:, row_index, :]
            .add(returned)
        )
        row_terms = row_terms.reshape(vector_count, band_rows)
        rows_own = (
            lax.psum_scatter(row_terms, "bkt", scatter_dimension=1, tiled=True) * inv_own[None, :]
        )
        gram_local = jnp.dot(rows_own, rows_own.T, precision=highest)
        gram_matrix = lax.psum(gram_local, ("doc", "bkt")) / total_docs
        factor = jnp.linalg.cholesky(gram_matrix)
        vectors = lax.linalg.triangular_solve(factor, rows_own, left_side=True, lower=True)
    return vectors


MESH = pl.DeviceIdType.MESH
F32 = jnp.float32
BF16 = jnp.bfloat16
NT = (((1,), (1,)), ((), ()))
BLOCK = 4


def kernel(
    nd,
    nb,
    slot_ref,
    start_ref,
    weight_ref,
    patterns_hbm,
    out_ref,
    tiles,
    dense,
    doc_part,
    doc_recv,
    size_part,
    size_recv,
    size_acc,
    weight_terms,
    band,
    panel_send,
    panel_recv,
    weighted,
    image_acc,
    pre_send,
    pre_recv,
    image_send,
    image_recv,
    gram_one,
    gram_one_recv,
    gram_two,
    gram_two_recv,
    load_sem,
    deg_send_sem,
    deg_recv_sem,
    size_send_sem,
    size_recv_sem,
    band_send_sem,
    band_recv_sem,
    panel_send_sem,
    panel_recv_sem,
    wt_send_sem,
    wt_recv_sem,
    pre_send_sem,
    pre_recv_sem,
    image_send_sem,
    image_recv_sem,
    g1_send_sem,
    g1_recv_sem,
    g2_send_sem,
    g2_recv_sem,
):
    highest = lax.Precision.HIGHEST
    me_d = lax.axis_index("doc")
    me_b = lax.axis_index("bkt")
    tile = tiles.shape[1]
    k_vec, own_rows = start_ref.shape
    own_cols = dense.shape[2]
    row_tiles = dense.shape[1] // tile
    col_per = own_cols // tile
    col_tiles = nd * col_per
    tiles_per_own = own_rows // tile
    total_docs = own_rows * nb * nd

    def d_peer(k):
        return {"doc": lax.rem(me_d + k, nd)}

    def b_peer(k):
        return {"bkt": lax.rem(me_b + k, nb)}

    slots = tiles.shape[0] - 1
    tiles[slots] = jnp.zeros((tile, tile), jnp.int32)
    load = pltpu.make_async_copy(patterns_hbm, tiles.at[pl.ds(0, slots)], load_sem)
    load.start()
    barrier = pltpu.get_barrier_semaphore()
    for k in range(1, nb):
        pl.semaphore_signal(barrier, inc=1, device_id=b_peer(k), device_id_type=MESH)
    for k in range(1, nd):
        pl.semaphore_signal(barrier, inc=1, device_id=d_peer(k), device_id_type=MESH)
    pl.semaphore_wait(barrier, nb + nd - 2)

    def remote(src, dst, ssem, rsem, peer):
        copy = pltpu.make_async_remote_copy(
            src_ref=src, dst_ref=dst, send_sem=ssem, recv_sem=rsem,
            device_id=peer, device_id_type=MESH,
        )
        copy.start()
        return copy

    half_b, half_d = nb // 2, nd // 2
    mate_b = me_b + 1 - 2 * lax.rem(me_b, 2)
    mate_d = me_d + 1 - 2 * lax.rem(me_d, 2)
    b_mate, d_mate = {"bkt": mate_b}, {"doc": mate_d}

    def b_far(j):
        return {"bkt": lax.rem(me_b + 2 * j, nb)}

    def d_far(j):
        return {"doc": lax.rem(me_d + 2 * j, nd)}

    def source_of(me, n, j, side):
        origin = me + 1 - 2 * lax.rem(me, 2) if side else me
        return lax.rem(origin - 2 * j + n, n)

    def gather_start(buf, ssem, rsem, half, far, mate):
        sent = {}
        for j in range(1, half):
            sent[(j, 0)] = remote(buf.at[0, 0], buf.at[j, 0], ssem.at[j, 0], rsem.at[j, 0], far(j))
        sent[(0, 1)] = remote(buf.at[0, 0], buf.at[0, 1], ssem.at[0, 1], rsem.at[0, 1], mate)
        return sent

    def gather_relay(buf, ssem, rsem, j, sent, mate):
        sent[(j, 0)].wait_recv()
        sent[(j, 1)] = remote(buf.at[j, 0], buf.at[j, 1], ssem.at[j, 1], rsem.at[j, 1], mate)

    def gather_rest(sent):
        for (j, side), copy in sent.items():
            if side:
                copy.wait_recv()
        for copy in sent.values():
            copy.wait_send()

    for o in range(nd):
        left = weight_ref[o]
        terms = []
        for _ in range(3):
            terms.append(left.astype(BF16))
            left = left - terms[-1].astype(F32)
        terms = [jnp.broadcast_to(term.astype(F32), (1, own_cols)) for term in terms]
        terms.append(jnp.zeros((13, own_cols), F32))
        weight_terms[o] = jnp.concatenate(terms, axis=0).astype(BF16)
    size_acc[...] = jnp.zeros_like(size_acc)
    group = 2 if tiles_per_own % 2 == 0 else 1
    load.wait()

    @pl.loop(0, row_tiles // group)
    def _(g):
        rows = pl.ds(pl.multiple_of(g * group * tile, group * tile), group * tile)
        total = jnp.zeros((16, group * tile), F32)
        for o in range(nd):
            for h in range(col_per):
                lanes = slice(h * tile, (h + 1) * tile)
                sums = size_acc[o, :, lanes]
                blocks = []
                for u in range(group):
                    at = (g * group + u) * col_tiles + o * col_per + h
                    block = tiles[slot_ref[at]].astype(F32)
                    sums = sums + jnp.sum(block.reshape(tile // 8, 8, tile), axis=0)
                    blocks.append(block.astype(BF16))
                size_acc[o, :, lanes] = sums
                dense[o, rows, lanes] = jnp.concatenate(blocks, axis=0)
            total = total + lax.dot_general(weight_terms[o], dense[o, rows, :], NT, preferred_element_type=F32)
        summed = total[0:1] + total[1:2] + total[2:3]
        at = g * group * tile
        doc_part[at // own_rows, :, pl.ds(pl.multiple_of(lax.rem(at, own_rows), group * tile), group * tile)] = summed

    for o in range(nd):
        size_part[o] = jnp.sum(size_acc[o], axis=0, keepdims=True)

    copies = []
    for k in range(1, nb):
        q = lax.rem(me_b + k, nb)
        copies.append(remote(doc_part.at[q], doc_recv.at[k], deg_send_sem.at[k], deg_recv_sem.at[k], b_peer(k)))
    for k in range(1, nd):
        o = lax.rem(me_d + k, nd)
        copies.append(remote(size_part.at[o], size_recv.at[k], size_send_sem.at[k], size_recv_sem.at[k], d_peer(k)))
    for copy in copies:
        copy.wait()
    degree = doc_part[me_b]
    for k in range(1, nb):
        degree = degree + doc_recv[k]
    size = size_part[me_d]
    for k in range(1, nd):
        size = size + size_recv[k]
    inv_own = 1.0 / jnp.sqrt(jnp.maximum(degree, 1.0))
    scale = weight_ref[me_d] / jnp.maximum(size, 1.0)

    vectors = start_ref[...]
    for it in range(ITERS):
        band[it, 0, 0] = (vectors * inv_own).astype(BF16)
        sent = gather_start(band.at[it], band_send_sem.at[it], band_recv_sem.at[it], half_b, b_far, b_mate)
        for j in range(1, half_b):
            gather_relay(band.at[it], band_send_sem.at[it], band_recv_sem.at[it], j, sent, b_mate)
        gather_rest(sent)

        def panel_of(o):
            acc = jnp.zeros((k_vec, own_cols), F32)
            for j in range(half_b):
                for side in range(2):
                    source = source_of(me_b, nb, j, side)
                    rows = pl.ds(pl.multiple_of(source * own_rows, own_rows), own_rows)
                    acc = acc + jnp.dot(band[it, j, side], dense[o, rows, :], preferred_element_type=F32)
            return acc

        @pl.loop(1, nd)
        def _(k):
            panel_send[it, k] = panel_of(lax.rem(me_d + k, nd)).astype(BF16)
            remote(panel_send.at[it, k], panel_recv.at[it, k], panel_send_sem.at[it, k], panel_recv_sem.at[it, k], d_peer(k))

        whole = panel_of(me_d)
        for k in range(1, nd):
            pltpu.make_async_remote_copy(
                src_ref=panel_send.at[it, k], dst_ref=panel_recv.at[it, k],
                send_sem=panel_send_sem.at[it, k], recv_sem=panel_recv_sem.at[it, k],
                device_id=d_peer(k), device_id_type=MESH,
            ).wait()
            whole = whole + panel_recv[it, k].astype(F32)
        weighted[it, 0, 0] = (whole * scale).astype(BF16)
        sent = gather_start(weighted.at[it], wt_send_sem.at[it], wt_recv_sem.at[it], half_d, d_far, d_mate)

        def term(q, j, side):
            rows = pl.ds(pl.multiple_of(q * own_rows, own_rows), own_rows)
            source = source_of(me_d, nd, j, side)
            return lax.dot_general(weighted[it, j, side], dense[source, rows, :], NT, preferred_element_type=F32)

        @pl.loop(0, nb)
        def _(q):
            image_acc[q] = term(q, 0, 0)

        for j in range(1, half_d):
            gather_relay(weighted.at[it], wt_send_sem.at[it], wt_recv_sem.at[it], j, sent, d_mate)
            sent[(j - 1, 1)].wait_recv()

            @pl.loop(0, nb)
            def _(q):
                image_acc[q] += term(q, j, 0) + term(q, j - 1, 1)

        last = (half_d - 1, 1)
        sent[last].wait_recv()
        for copy in sent.values():
            copy.wait_send()

        def finish(q):
            return image_acc[q] + term(q, *last)

        pre = {}
        for j in range(1, half_b):
            pre_send[it, j] = finish(lax.rem(mate_b + 2 * j, nb)).astype(BF16)
            pre[j] = remote(pre_send.at[it, j], pre_recv.at[it, j], pre_send_sem.at[it, j], pre_recv_sem.at[it, j], b_mate)
        out = []
        for j in range(1, half_b):
            both = finish(lax.rem(me_b + 2 * j, nb))
            pre[j].wait()
            image_send[it, j] = (both + pre_recv[it, j].astype(F32)).astype(BF16)
            out.append(remote(image_send.at[it, j], image_recv.at[it, j], image_send_sem.at[it, j], image_recv_sem.at[it, j], b_far(j)))
        pre_send[it, 0] = finish(mate_b).astype(BF16)
        mine = remote(pre_send.at[it, 0], pre_recv.at[it, 0], pre_send_sem.at[it, 0], pre_recv_sem.at[it, 0], b_mate)
        image = finish(me_b)
        mine.wait()
        image = image + pre_recv[it, 0].astype(F32)
        for j in range(1, half_b):
            out[j - 1].wait()
            image = image + image_recv[it, j].astype(F32)
        image = image * inv_own

        gram = lax.dot_general(image, image, NT, precision=highest, preferred_element_type=F32)
        half = k_vec // 2
        gram_one[it] = jnp.concatenate([gram[:half], gram[half:]], axis=1)
        sent = [
            remote(gram_one.at[it], gram_one_recv.at[it, k], g1_send_sem.at[it, k], g1_recv_sem.at[it, k], b_peer(k))
            for k in range(1, nb)
        ]
        folded = gram_one[it]
        for k in range(1, nb):
            sent[k - 1].wait()
            folded = folded + gram_one_recv[it, k]
        gram_two[it] = folded
        sent = [
            remote(gram_two.at[it], gram_two_recv.at[it, k], g2_send_sem.at[it, k], g2_recv_sem.at[it, k], d_peer(k))
            for k in range(1, nd)
        ]
        for k in range(1, nd):
            sent[k - 1].wait()
            folded = folded + gram_two_recv[it, k]
        gram = jnp.concatenate([folded[:, :k_vec], folded[:, k_vec:]], axis=0) / total_docs

        row_at = lax.broadcasted_iota(jnp.int32, (k_vec, k_vec), 0)
        col_at = lax.broadcasted_iota(jnp.int32, (k_vec, k_vec), 1)
        eye = (row_at == col_at).astype(F32)
        work = jnp.concatenate([gram, eye], axis=1)
        for at in range(0, k_vec, BLOCK):
            top = at // 8 * 8
            part = work[top:]
            below = lax.broadcasted_iota(jnp.int32, part.shape, 0)
            cols = [jnp.broadcast_to(part[:, at + m : at + m + 1], part.shape) for m in range(BLOCK)]
            for m in range(BLOCK):
                row = at - top + m
                factor = jnp.where(below > row, cols[m] * (1.0 / cols[m][row : row + 1]), 0.0)
                part = part - factor * part[row : row + 1]
                for n in range(m + 1, BLOCK):
                    cols[n] = cols[n] - factor * cols[n][row : row + 1]
            work = jnp.concatenate([work[:top], part], axis=0) if top else part
        pivots = jnp.sum(work[:, :k_vec] * eye, axis=1, keepdims=True)
        inverse = work[:, k_vec:] / jnp.sqrt(pivots)
        vectors = jnp.dot(inverse, image, precision=highest, preferred_element_type=F32)
    out_ref[...] = vectors


def scratch_of(nd, nb, slots, tile, k_vec, own_rows, own_cols):
    dma = pltpu.SemaphoreType.DMA
    vmem = pltpu.VMEM
    fold = (k_vec // 2, 2 * k_vec)
    buffers = [
        ((slots + 1, tile, tile), jnp.int32),
        ((nd, own_rows * nb, own_cols), BF16),
        ((nb, 1, own_rows), F32),
        ((nb, 1, own_rows), F32),
        ((nd, 1, own_cols), F32),
        ((nd, 1, own_cols), F32),
        ((nd, 8, own_cols), F32),
        ((nd, 16, own_cols), BF16),
        ((ITERS, nb // 2, 2, k_vec, own_rows), BF16),
        ((ITERS, nd, k_vec, own_cols), BF16),
        ((ITERS, nd, k_vec, own_cols), BF16),
        ((ITERS, nd // 2, 2, k_vec, own_cols), BF16),
        ((nb, k_vec, own_rows), F32),
        ((ITERS, nb // 2, k_vec, own_rows), BF16),
        ((ITERS, nb // 2, k_vec, own_rows), BF16),
        ((ITERS, nb // 2, k_vec, own_rows), BF16),
        ((ITERS, nb // 2, k_vec, own_rows), BF16),
        ((ITERS,) + fold, F32),
        ((ITERS, nb) + fold, F32),
        ((ITERS,) + fold, F32),
        ((ITERS, nd) + fold, F32),
    ]
    total = 0
    for shape, kind in buffers:
        count = jnp.dtype(kind).itemsize
        for extent in shape:
            count *= extent
        total += count
    sems = [dma]
    sems += [dma((nb,))] * 2 + [dma((nd,))] * 2
    sems += [dma((ITERS, nb // 2, 2))] * 2 + [dma((ITERS, nd))] * 2 + [dma((ITERS, nd // 2, 2))] * 2
    sems += [dma((ITERS, nb // 2))] * 4 + [dma((ITERS, nb))] * 2 + [dma((ITERS, nd))] * 2
    return [vmem(shape, kind) for shape, kind in buffers] + sems, total


VMEM_BYTES = 60000 * 1024


def body(start_vectors, bucket_weight, tile_count, tile_coords, patterns):
    nd, nb = lax.axis_size("doc"), lax.axis_size("bkt")
    slots, tile = patterns.shape[2], patterns.shape[3]
    k_vec, own_rows = start_vectors.shape
    band_cols = bucket_weight.shape[0]
    own_cols = band_cols // nd
    scratch, total = scratch_of(nd, nb, slots, tile, k_vec, own_rows, own_cols)
    fits = total + 6 * k_vec * own_rows * 4 < VMEM_BYTES
    even = nd % 2 == 0 and nb % 2 == 0 and band_cols % (nd * tile) == 0 and own_rows % tile == 0 and 2 * k_vec == tile
    if not (fits and even):
        return plain_body(start_vectors, bucket_weight, tile_count, tile_coords, patterns)
    row_tiles, col_tiles = own_rows * nb // tile, band_cols // tile
    places = tile_coords[0, 0, :, 0] * col_tiles + tile_coords[0, 0, :, 1]
    slot_ids = jnp.arange(slots)
    places = jnp.where(slot_ids < tile_count[0, 0], places, -1)
    match = jnp.arange(row_tiles * col_tiles)[:, None] == places[None, :]
    found = jnp.max(jnp.where(match, slot_ids[None, :], -1), axis=1)
    slot_of = jnp.where(found >= 0, found, slots).astype(jnp.int32)
    smem = pl.BlockSpec(memory_space=pltpu.SMEM)
    vmem = pl.BlockSpec(memory_space=pltpu.VMEM)
    return pl.pallas_call(
        functools.partial(kernel, nd, nb),
        out_shape=jax.ShapeDtypeStruct((k_vec, own_rows), F32),
        in_specs=[smem, vmem, vmem, pl.BlockSpec(memory_space=pl.ANY)],
        out_specs=vmem,
        scratch_shapes=scratch,
        compiler_params=pltpu.CompilerParams(
            collective_id=0, has_side_effects=True, vmem_limit_bytes=VMEM_BYTES
        ),
        name="subspace",
    )(slot_of, start_vectors, bucket_weight.reshape(nd, 1, own_cols), patterns.reshape(slots, tile, tile))


def solution(mesh):
    in_specs = (
        P(None, ("doc", "bkt")),
        P("bkt"),
        P("doc", "bkt"),
        P("doc", "bkt", None, None),
        P("doc", "bkt", None, None, None),
    )
    out_specs = P(None, ("doc", "bkt"))
    return jax.shard_map(body, mesh=mesh, in_specs=in_specs, out_specs=out_specs, check_vma=False)
```

```python
import functools

import jax
import jax.numpy as jnp
from jax import lax
from jax.experimental import pallas as pl
from jax.experimental.pallas import tpu as pltpu
from jax.sharding import PartitionSpec as P

ITERS = 2


def plain_body(start_vectors, bucket_weight, tile_count, tile_coords, patterns):
    highest = lax.Precision.HIGHEST
    slot_total = patterns.shape[2]
    tile_size = patterns.shape[3]
    vector_count = start_vectors.shape[0]
    own_rows = start_vectors.shape[1]
    band_rows = own_rows * lax.axis_size("bkt")
    band_cols = bucket_weight.shape[0]
    row_tiles = band_rows // tile_size
    col_tiles = band_cols // tile_size
    total_docs = band_rows * lax.axis_size("doc")
    live_slot = (jnp.arange(slot_total) < tile_count[0, 0]).astype(jnp.int32)
    pattern_int = patterns[0, 0] * live_slot[:, None, None]
    pattern = pattern_int.astype(jnp.bfloat16)
    row_index = tile_coords[0, 0, :, 0]
    col_index = tile_coords[0, 0, :, 1]
    row_pick = jnp.arange(row_tiles)[:, None] == row_index[None, :]
    col_pick = jnp.arange(col_tiles)[:, None] == col_index[None, :]
    row_pick_f = row_pick.astype(jnp.float32)
    row_pick_b = row_pick.astype(jnp.bfloat16)
    col_pick_f = col_pick.astype(jnp.float32)
    col_pick_b = col_pick.astype(jnp.bfloat16)
    pattern_f = pattern_int.astype(jnp.float32)
    weight_tiles = bucket_weight.reshape(col_tiles, tile_size)
    slot_weight = jnp.dot(col_pick_f.T, weight_tiles, precision=highest)
    row_part = jnp.einsum("tij,tj->ti", pattern_f, slot_weight, precision=highest)
    doc_part = jnp.dot(row_pick_f, row_part, precision=highest).reshape(band_rows)
    col_part = jnp.sum(pattern_f, axis=1)
    bucket_part = jnp.dot(col_pick_f, col_part, precision=highest).reshape(band_cols)
    doc_degree = lax.psum(doc_part, "bkt")
    bucket_size = lax.psum(bucket_part.astype(jnp.bfloat16), "doc").astype(jnp.float32)
    inv_band = 1.0 / jnp.sqrt(jnp.maximum(doc_degree, 1.0))
    inv_own = lax.dynamic_slice_in_dim(inv_band, lax.axis_index("bkt") * own_rows, own_rows)
    bucket_scale = bucket_weight / jnp.maximum(bucket_size, 1.0)
    vectors = start_vectors
    for sweep_index in range(ITERS):
        scaled = (vectors * inv_own[None, :]).astype(jnp.bfloat16)
        band_vecs = lax.all_gather(scaled, "bkt", axis=1, tiled=True)
        picked = jnp.einsum(
            "rt,kri->kti",
            row_pick_b,
            band_vecs.reshape(vector_count, row_tiles, tile_size),
            preferred_element_type=jnp.float32,
        ).astype(jnp.bfloat16)
        products = jnp.einsum("kti,tij->ktj", picked, pattern, preferred_element_type=jnp.float32)
        panel_part = (
            jnp.zeros((vector_count, col_tiles, tile_size), jnp.float32)
            .at[:, col_index, :]
            .add(products)
        )
        panel_part = panel_part.reshape(vector_count, band_cols)
        panel_whole = lax.psum(panel_part, "doc")
        weighted = (panel_whole * bucket_scale[None, :]).astype(jnp.bfloat16)
        spread = jnp.einsum(
            "ct,kcj->ktj",
            col_pick_b,
            weighted.reshape(vector_count, col_tiles, tile_size),
            preferred_element_type=jnp.float32,
        ).astype(jnp.bfloat16)
        returned = jnp.einsum("ktj,tij->kti", spread, pattern, preferred_element_type=jnp.float32)
        row_terms = (
            jnp.zeros((vector_count, row_tiles, tile_size), jnp.float32)
            .at[:, row_index, :]
            .add(returned)
        )
        row_terms = row_terms.reshape(vector_count, band_rows)
        rows_own = (
            lax.psum_scatter(row_terms, "bkt", scatter_dimension=1, tiled=True) * inv_own[None, :]
        )
        gram_local = jnp.dot(rows_own, rows_own.T, precision=highest)
        gram_matrix = lax.psum(gram_local, ("doc", "bkt")) / total_docs
        factor = jnp.linalg.cholesky(gram_matrix)
        vectors = lax.linalg.triangular_solve(factor, rows_own, left_side=True, lower=True)
    return vectors


MESH = pl.DeviceIdType.MESH
F32 = jnp.float32
BF16 = jnp.bfloat16
NT = (((1,), (1,)), ((), ()))
BLOCK = 4


def kernel(
    nd,
    nb,
    slot_ref,
    start_ref,
    weight_ref,
    patterns_hbm,
    out_ref,
    tiles,
    dense,
    doc_part,
    doc_recv,
    size_part,
    size_recv,
    size_acc,
    weight_terms,
    band,
    panel_send,
    panel_recv,
    weighted,
    image_acc,
    pre_send,
    pre_recv,
    image_send,
    image_recv,
    gram_one,
    gram_one_recv,
    gram_two,
    gram_two_recv,
    inv_all,
    full,
    load_sem,
    deg_send_sem,
    deg_recv_sem,
    size_send_sem,
    size_recv_sem,
    band_send_sem,
    band_recv_sem,
    panel_send_sem,
    panel_recv_sem,
    wt_send_sem,
    wt_recv_sem,
    pre_send_sem,
    pre_recv_sem,
    image_send_sem,
    image_recv_sem,
    g1_send_sem,
    g1_recv_sem,
    g2_send_sem,
    g2_recv_sem,
    inv_send_sem,
    inv_recv_sem,
    full_send_sem,
    full_recv_sem,
):
    highest = lax.Precision.HIGHEST
    me_d = lax.axis_index("doc")
    me_b = lax.axis_index("bkt")
    tile = tiles.shape[1]
    k_vec, own_rows = start_ref.shape
    own_cols = dense.shape[2]
    row_tiles = dense.shape[1] // tile
    col_per = own_cols // tile
    col_tiles = nd * col_per
    tiles_per_own = own_rows // tile
    total_docs = own_rows * nb * nd

    def d_peer(k):
        return {"doc": lax.rem(me_d + k, nd)}

    def b_peer(k):
        return {"bkt": lax.rem(me_b + k, nb)}

    slots = tiles.shape[0] - 1
    tiles[slots] = jnp.zeros((tile, tile), jnp.int32)
    load = pltpu.make_async_copy(patterns_hbm, tiles.at[pl.ds(0, slots)], load_sem)
    load.start()
    barrier = pltpu.get_barrier_semaphore()
    for k in range(1, nb):
        pl.semaphore_signal(barrier, inc=1, device_id=b_peer(k), device_id_type=MESH)
    for k in range(1, nd):
        pl.semaphore_signal(barrier, inc=1, device_id=d_peer(k), device_id_type=MESH)
    pl.semaphore_wait(barrier, nb + nd - 2)

    def remote(src, dst, ssem, rsem, peer):
        copy = pltpu.make_async_remote_copy(
            src_ref=src, dst_ref=dst, send_sem=ssem, recv_sem=rsem,
            device_id=peer, device_id_type=MESH,
        )
        copy.start()
        return copy

    half_b, half_d = nb // 2, nd // 2
    mate_b = me_b + 1 - 2 * lax.rem(me_b, 2)
    mate_d = me_d + 1 - 2 * lax.rem(me_d, 2)
    b_mate, d_mate = {"bkt": mate_b}, {"doc": mate_d}

    def b_far(j):
        return {"bkt": lax.rem(me_b + 2 * j, nb)}

    def d_far(j):
        return {"doc": lax.rem(me_d + 2 * j, nd)}

    def source_of(me, n, j, side):
        origin = me + 1 - 2 * lax.rem(me, 2) if side else me
        return lax.rem(origin - 2 * j + n, n)

    def gather_start(buf, ssem, rsem, half, far, mate):
        sent = {}
        for j in range(1, half):
            sent[(j, 0)] = remote(buf.at[0, 0], buf.at[j, 0], ssem.at[j, 0], rsem.at[j, 0], far(j))
        sent[(0, 1)] = remote(buf.at[0, 0], buf.at[0, 1], ssem.at[0, 1], rsem.at[0, 1], mate)
        return sent

    def gather_relay(buf, ssem, rsem, j, sent, mate):
        sent[(j, 0)].wait_recv()
        sent[(j, 1)] = remote(buf.at[j, 0], buf.at[j, 1], ssem.at[j, 1], rsem.at[j, 1], mate)

    def gather_rest(sent):
        for (j, side), copy in sent.items():
            if side:
                copy.wait_recv()
        for copy in sent.values():
            copy.wait_send()

    for o in range(nd):
        left = weight_ref[o]
        terms = []
        for _ in range(3):
            terms.append(left.astype(BF16))
            left = left - terms[-1].astype(F32)
        terms = [jnp.broadcast_to(term.astype(F32), (1, own_cols)) for term in terms]
        terms.append(jnp.zeros((13, own_cols), F32))
        weight_terms[o] = jnp.concatenate(terms, axis=0).astype(BF16)
    size_acc[...] = jnp.zeros_like(size_acc)
    group = 2 if tiles_per_own % 2 == 0 else 1
    load.wait()

    @pl.loop(0, row_tiles // group)
    def _(g):
        rows = pl.ds(pl.multiple_of(g * group * tile, group * tile), group * tile)
        total = jnp.zeros((16, group * tile), F32)
        for o in range(nd):
            for h in range(col_per):
                lanes = slice(h * tile, (h + 1) * tile)
                sums = size_acc[o, :, lanes]
                blocks = []
                for u in range(group):
                    at = (g * group + u) * col_tiles + o * col_per + h
                    block = tiles[slot_ref[at]].astype(F32)
                    sums = sums + jnp.sum(block.reshape(tile // 8, 8, tile), axis=0)
                    blocks.append(block.astype(BF16))
                size_acc[o, :, lanes] = sums
                dense[o, rows, lanes] = jnp.concatenate(blocks, axis=0)
            total = total + lax.dot_general(weight_terms[o], dense[o, rows, :], NT, preferred_element_type=F32)
        summed = total[0:1] + total[1:2] + total[2:3]
        at = g * group * tile
        doc_part[at // own_rows, :, pl.ds(pl.multiple_of(lax.rem(at, own_rows), group * tile), group * tile)] = summed

    for o in range(nd):
        size_part[o] = jnp.sum(size_acc[o], axis=0, keepdims=True)

    copies = []
    for k in range(1, nb):
        q = lax.rem(me_b + k, nb)
        copies.append(remote(doc_part.at[q], doc_recv.at[k], deg_send_sem.at[k], deg_recv_sem.at[k], b_peer(k)))
    for k in range(1, nd):
        o = lax.rem(me_d + k, nd)
        copies.append(remote(size_part.at[o], size_recv.at[k], size_send_sem.at[k], size_recv_sem.at[k], d_peer(k)))
    for copy in copies:
        copy.wait()
    degree = doc_part[me_b]
    for k in range(1, nb):
        degree = degree + doc_recv[k]
    size = size_part[me_d]
    for k in range(1, nd):
        size = size + size_recv[k]
    inv_own = 1.0 / jnp.sqrt(jnp.maximum(degree, 1.0))
    scale = weight_ref[me_d] / jnp.maximum(size, 1.0)

    inv_all[me_b] = inv_own
    inv_sent = [
        remote(inv_all.at[me_b], inv_all.at[me_b], inv_send_sem.at[k], inv_recv_sem.at[k], b_peer(k))
        for k in range(1, nb)
    ]

    band[0, 0, 0] = (start_ref[...] * inv_own).astype(BF16)
    sent = gather_start(band.at[0], band_send_sem.at[0], band_recv_sem.at[0], half_b, b_far, b_mate)
    for j in range(1, half_b):
        gather_relay(band.at[0], band_send_sem.at[0], band_recv_sem.at[0], j, sent, b_mate)
    gather_rest(sent)
    for copy in inv_sent:
        copy.wait()

    for it in range(ITERS):
        def panel_of(o):
            acc = jnp.zeros((k_vec, own_cols), F32)
            for j in range(half_b):
                for side in range(2):
                    source = source_of(me_b, nb, j, side)
                    rows = pl.ds(pl.multiple_of(source * own_rows, own_rows), own_rows)
                    acc = acc + jnp.dot(band[it, j, side], dense[o, rows, :], preferred_element_type=F32)
            return acc

        @pl.loop(1, nd)
        def _(k):
            panel_send[it, k] = panel_of(lax.rem(me_d + k, nd)).astype(BF16)
            remote(panel_send.at[it, k], panel_recv.at[it, k], panel_send_sem.at[it, k], panel_recv_sem.at[it, k], d_peer(k))

        whole = panel_of(me_d)
        for k in range(1, nd):
            pltpu.make_async_remote_copy(
                src_ref=panel_send.at[it, k], dst_ref=panel_recv.at[it, k],
                send_sem=panel_send_sem.at[it, k], recv_sem=panel_recv_sem.at[it, k],
                device_id=d_peer(k), device_id_type=MESH,
            ).wait()
            whole = whole + panel_recv[it, k].astype(F32)
        weighted[it, 0, 0] = (whole * scale).astype(BF16)
        sent = gather_start(weighted.at[it], wt_send_sem.at[it], wt_recv_sem.at[it], half_d, d_far, d_mate)

        def term(q, j, side):
            rows = pl.ds(pl.multiple_of(q * own_rows, own_rows), own_rows)
            source = source_of(me_d, nd, j, side)
            return lax.dot_general(weighted[it, j, side], dense[source, rows, :], NT, preferred_element_type=F32)

        @pl.loop(0, nb)
        def _(q):
            image_acc[q] = term(q, 0, 0)

        for j in range(1, half_d):
            gather_relay(weighted.at[it], wt_send_sem.at[it], wt_recv_sem.at[it], j, sent, d_mate)
            sent[(j - 1, 1)].wait_recv()

            @pl.loop(0, nb)
            def _(q):
                image_acc[q] += term(q, j, 0) + term(q, j - 1, 1)

        last = (half_d - 1, 1)
        sent[last].wait_recv()
        for copy in sent.values():
            copy.wait_send()

        def finish(q):
            return image_acc[q] + term(q, *last)

        pre = {}
        for j in range(1, half_b):
            pre_send[it, j] = finish(lax.rem(mate_b + 2 * j, nb)).astype(BF16)
            pre[j] = remote(pre_send.at[it, j], pre_recv.at[it, j], pre_send_sem.at[it, j], pre_recv_sem.at[it, j], b_mate)
        out = []
        for j in range(1, half_b):
            both = finish(lax.rem(me_b + 2 * j, nb))
            pre[j].wait()
            image_send[it, j] = (both + pre_recv[it, j].astype(F32)).astype(BF16)
            out.append(remote(image_send.at[it, j], image_recv.at[it, j], image_send_sem.at[it, j], image_recv_sem.at[it, j], b_far(j)))
        pre_send[it, 0] = finish(mate_b).astype(BF16)
        mine = remote(pre_send.at[it, 0], pre_recv.at[it, 0], pre_send_sem.at[it, 0], pre_recv_sem.at[it, 0], b_mate)
        image = finish(me_b)
        mine.wait()
        image = image + pre_recv[it, 0].astype(F32)
        for j in range(1, half_b):
            out[j - 1].wait()
            image = image + image_recv[it, j].astype(F32)
        image = image * inv_own

        gram = lax.dot_general(image, image, NT, precision=highest, preferred_element_type=F32)
        half = k_vec // 2
        gram_one[it] = jnp.concatenate([gram[:half], gram[half:]], axis=1)
        sent = [
            remote(gram_one.at[it], gram_one_recv.at[it, k], g1_send_sem.at[it, k], g1_recv_sem.at[it, k], b_peer(k))
            for k in range(1, nb)
        ]
        folded = gram_one[it]
        for k in range(1, nb):
            sent[k - 1].wait()
            folded = folded + gram_one_recv[it, k]
        gram_two[it] = folded
        more = it + 1 < ITERS
        if more:
            full[it, 0, 0] = image
            gather = gather_start(full.at[it], full_send_sem.at[it], full_recv_sem.at[it], half_b, b_far, b_mate)
        sent = [
            remote(gram_two.at[it], gram_two_recv.at[it, k], g2_send_sem.at[it, k], g2_recv_sem.at[it, k], d_peer(k))
            for k in range(1, nd)
        ]
        for k in range(1, nd):
            sent[k - 1].wait()
            folded = folded + gram_two_recv[it, k]
        if more:
            for j in range(1, half_b):
                gather_relay(full.at[it], full_send_sem.at[it], full_recv_sem.at[it], j, gather, b_mate)
        gram = jnp.concatenate([folded[:, :k_vec], folded[:, k_vec:]], axis=0) / total_docs

        row_at = lax.broadcasted_iota(jnp.int32, (k_vec, k_vec), 0)
        col_at = lax.broadcasted_iota(jnp.int32, (k_vec, k_vec), 1)
        eye = (row_at == col_at).astype(F32)
        work = jnp.concatenate([gram, eye], axis=1)
        for at in range(0, k_vec, BLOCK):
            top = at // 8 * 8
            part = work[top:]
            below = lax.broadcasted_iota(jnp.int32, part.shape, 0)
            cols = [jnp.broadcast_to(part[:, at + m : at + m + 1], part.shape) for m in range(BLOCK)]
            for m in range(BLOCK):
                row = at - top + m
                factor = jnp.where(below > row, cols[m] * (1.0 / cols[m][row : row + 1]), 0.0)
                part = part - factor * part[row : row + 1]
                for n in range(m + 1, BLOCK):
                    cols[n] = cols[n] - factor * cols[n][row : row + 1]
            work = jnp.concatenate([work[:top], part], axis=0) if top else part
        pivots = jnp.sum(work[:, :k_vec] * eye, axis=1, keepdims=True)
        inverse = work[:, k_vec:] / jnp.sqrt(pivots)
        if more:
            for j in range(half_b):
                for side in range(2):
                    if side:
                        gather[(j, side)].wait_recv()
                    vectors = jnp.dot(inverse, full[it, j, side], precision=highest, preferred_element_type=F32)
                    band[it + 1, j, side] = (vectors * inv_all[source_of(me_b, nb, j, side)]).astype(BF16)
            for copy in gather.values():
                copy.wait_send()
        else:
            out_ref[...] = jnp.dot(inverse, image, precision=highest, preferred_element_type=F32)


def scratch_of(nd, nb, slots, tile, k_vec, own_rows, own_cols):
    dma = pltpu.SemaphoreType.DMA
    vmem = pltpu.VMEM
    fold = (k_vec // 2, 2 * k_vec)
    buffers = [
        ((slots + 1, tile, tile), jnp.int32),
        ((nd, own_rows * nb, own_cols), BF16),
        ((nb, 1, own_rows), F32),
        ((nb, 1, own_rows), F32),
        ((nd, 1, own_cols), F32),
        ((nd, 1, own_cols), F32),
        ((nd, 8, own_cols), F32),
        ((nd, 16, own_cols), BF16),
        ((ITERS, nb // 2, 2, k_vec, own_rows), BF16),
        ((ITERS, nd, k_vec, own_cols), BF16),
        ((ITERS, nd, k_vec, own_cols), BF16),
        ((ITERS, nd // 2, 2, k_vec, own_cols), BF16),
        ((nb, k_vec, own_rows), F32),
        ((ITERS, nb // 2, k_vec, own_rows), BF16),
        ((ITERS, nb // 2, k_vec, own_rows), BF16),
        ((ITERS, nb // 2, k_vec, own_rows), BF16),
        ((ITERS, nb // 2, k_vec, own_rows), BF16),
        ((ITERS,) + fold, F32),
        ((ITERS, nb) + fold, F32),
        ((ITERS,) + fold, F32),
        ((ITERS, nd) + fold, F32),
        ((nb, 1, own_rows), F32),
        ((ITERS, nb // 2, 2, k_vec, own_rows), F32),
    ]
    total = 0
    for shape, kind in buffers:
        count = jnp.dtype(kind).itemsize
        for extent in shape:
            count *= extent
        total += count
    sems = [dma]
    sems += [dma((nb,))] * 2 + [dma((nd,))] * 2
    sems += [dma((ITERS, nb // 2, 2))] * 2 + [dma((ITERS, nd))] * 2 + [dma((ITERS, nd // 2, 2))] * 2
    last = [dma((nb,))] * 2 + [dma((ITERS, nb // 2, 2))] * 2
    sems += [dma((ITERS, nb // 2))] * 4 + [dma((ITERS, nb))] * 2 + [dma((ITERS, nd))] * 2 + last
    return [vmem(shape, kind) for shape, kind in buffers] + sems, total


VMEM_BYTES = 60000 * 1024


def body(start_vectors, bucket_weight, tile_count, tile_coords, patterns):
    nd, nb = lax.axis_size("doc"), lax.axis_size("bkt")
    slots, tile = patterns.shape[2], patterns.shape[3]
    k_vec, own_rows = start_vectors.shape
    band_cols = bucket_weight.shape[0]
    own_cols = band_cols // nd
    scratch, total = scratch_of(nd, nb, slots, tile, k_vec, own_rows, own_cols)
    fits = total + 6 * k_vec * own_rows * 4 < VMEM_BYTES
    even = nd % 2 == 0 and nb % 2 == 0 and band_cols % (nd * tile) == 0 and own_rows % tile == 0 and 2 * k_vec == tile
    if not (fits and even):
        return plain_body(start_vectors, bucket_weight, tile_count, tile_coords, patterns)
    row_tiles, col_tiles = own_rows * nb // tile, band_cols // tile
    places = tile_coords[0, 0, :, 0] * col_tiles + tile_coords[0, 0, :, 1]
    slot_ids = jnp.arange(slots)
    places = jnp.where(slot_ids < tile_count[0, 0], places, -1)
    match = jnp.arange(row_tiles * col_tiles)[:, None] == places[None, :]
    found = jnp.max(jnp.where(match, slot_ids[None, :], -1), axis=1)
    slot_of = jnp.where(found >= 0, found, slots).astype(jnp.int32)
    smem = pl.BlockSpec(memory_space=pltpu.SMEM)
    vmem = pl.BlockSpec(memory_space=pltpu.VMEM)
    return pl.pallas_call(
        functools.partial(kernel, nd, nb),
        out_shape=jax.ShapeDtypeStruct((k_vec, own_rows), F32),
        in_specs=[smem, vmem, vmem, pl.BlockSpec(memory_space=pl.ANY)],
        out_specs=vmem,
        scratch_shapes=scratch,
        compiler_params=pltpu.CompilerParams(
            collective_id=0, has_side_effects=True, vmem_limit_bytes=VMEM_BYTES
        ),
        name="subspace",
    )(slot_of, start_vectors, bucket_weight.reshape(nd, 1, own_cols), patterns.reshape(slots, tile, tile))


def solution(mesh):
    in_specs = (
        P(None, ("doc", "bkt")),
        P("bkt"),
        P("doc", "bkt"),
        P("doc", "bkt", None, None),
        P("doc", "bkt", None, None, None),
    )
    out_specs = P(None, ("doc", "bkt"))
    return jax.shard_map(body, mesh=mesh, in_specs=in_specs, out_specs=out_specs, check_vma=False)
```
